32 devices in a mesh: parts: 2 (over y), seq: 4 (over z), strand: 2 (over core), mp: 2 (over x).
Axes of the slice: x: 2, y: 2, z: 4, core: 2. Of those that a mesh axis runs over, the one named last changes fastest.
Arguments:
- hidden: bfloat16 [4096, 1024], P(('parts', 'seq'), 'mp'), parts along dimension 0, may hold values from -6 to 6
- breaks: int32 [4096], P('parts'), parts along dimension 0, may hold values 0 or 1
- cotangent: bfloat16 [4096, 1024], P(('parts', 'seq'), 'mp'), parts along dimension 0, may hold values from -0.059814453 to 0.059814453
- input_weight: bfloat16 [1024, 2048], P(('seq', 'strand'), 'mp'), may hold values from -0.1875 to 0.1875
- gate_weight: bfloat16 [1024, 2048], P(('seq', 'strand'), 'mp'), may hold values from -0.1875 to 0.1875
- key_weight: bfloat16 [1024, 1024], P(('seq', 'strand'), 'mp'), may hold values from -0.0625 to 0.0625
- query_weight: bfloat16 [1024, 1024], P(('seq', 'strand'), 'mp'), may hold values from -0.0625 to 0.0625
- step_weight: bfloat16 [1024, 32], P(('seq', 'strand'), 'mp'), may hold values from -0.1875 to 0.1875
- output_weight: bfloat16 [1024, 2048], P(('seq', 'strand'), 'mp'), may hold values from -0.125 to 0.125
- step_bias: float32 [32], P('mp'), may hold values from -4.5 to -2
- decay_log: float32 [32], P('mp'), may hold values from -13 to 0
- skip_gain: float32 [32], P('mp'), may hold values from 0.5 to 2
Outputs:
- combined: bfloat16 [4096, 1024], P(('parts', 'seq'), 'mp'), parts along dimension 0
- grad_input: float32 [2048, 2048], P(('parts', 'seq', 'strand'), 'mp'), parts along dimension 0
- grad_gate: float32 [2048, 2048], P(('parts', 'seq', 'strand'), 'mp'), parts along dimension 0
- grad_key: float32 [2048, 1024], P(('parts', 'seq', 'strand'), 'mp'), parts along dimension 0
- grad_query: float32 [2048, 1024], P(('parts', 'seq', 'strand'), 'mp'), parts along dimension 0
- grad_step: float32 [2048, 32], P(('parts', 'seq', 'strand'), 'mp'), parts along dimension 0
- grad_output: float32 [2048, 2048], P(('parts', 'seq', 'strand'), 'mp'), parts along dimension 0
The draws below stay inside these ranges and needn't reach their ends.
There are 2 independent parts, one for each index of `parts`. The reference program is written for one: setup_inputs(seed, part) draws one part's arguments, and reference() takes and returns one part's arrays. A program takes and returns all parts, laid end to end along the dimension named above; an argument that names none is the same for every part. Nothing has to cross between parts.
All inputs are finite; a program needn't handle non-finite values.
Results may differ from the reference program's by a relative error of at most 0.02.
Values may be sent and summed in bfloat16 or wider, within the bound.
A program may use at most 128 MiB of HBM per device.

```python
import math
from functools import partial
import jax
import jax.numpy as jnp
from jax import lax

D = 1024
HEADS = 32
HEAD_DIM = 64
STATE = 128
GROUPS = 8
STRETCH = 256
TOK_DEV = 512
INNER = 2048
SEQ_LEN = 2048
N_MP = 2


def draw_decay_log(key, part):
    key_pick, key_slow, key_fast = jax.random.split(key, 3)
    fast_share = 0.5
    is_fast = jax.random.uniform(key_pick, (HEADS,), jnp.float32) < fast_share
    slow_rate = jax.random.uniform(key_slow, (HEADS,), jnp.float32, math.log(0.2 / SEQ_LEN), math.log(5.0 / SEQ_LEN))
    fast_rate = jax.random.uniform(key_fast, (HEADS,), jnp.float32, math.log(0.15), math.log(0.6))
    return jnp.where(is_fast, fast_rate, slow_rate).astype(jnp.float32)


def set_ends(entries, stream_key, least, largest):
    longest = entries.shape.index(max(entries.shape))
    spots = []
    for shift in (0, 1):
        where = [jax.random.randint(jax.random.fold_in(stream_key, axis), (), 0, length) for axis, length in enumerate(entries.shape)]
        where[longest] = (where[longest] + shift) % entries.shape[longest]
        spots.append(tuple(where))
    return entries.at[spots[0]].set(least).at[spots[1]].set(largest)


def block_scale(rng, extent, cuts, least, top_value):
    factor_of, own = 1.0, jax.random.fold_in(rng, 6)
    for position, shards_of in cuts:
        heights = jnp.exp(jax.random.uniform(jax.random.fold_in(own, position), (shards_of,), jnp.float32, least / len(cuts), top_value / len(cuts)))
        factor_of = factor_of * jnp.repeat(heights, extent[position] // shards_of).reshape([-1 if axis == position else 1 for axis in range(len(extent))])
    return factor_of


def noise(rng, shape, deviation, limit, cuts=(), kind=jnp.bfloat16):
    gain = block_scale(rng, shape, cuts, -0.22, 0.18) if cuts else 1.0
    entries = jax.random.normal(rng, shape, jnp.float32) * deviation * gain
    return jnp.minimum(jnp.maximum(entries, -limit), limit).astype(kind)


def setup_inputs(seed: int = 0, part: int = 0) -> dict:
    key_list = jax.random.split(jax.random.key(seed), 13)
    part_keys = jax.random.split(jax.random.fold_in(key_list[12], part), 13)
    hidden = noise(part_keys[0], (SEQ_LEN, D), 1.0, 6.0, ((0, 4), (1, 2)))
    breaks = set_ends((jax.random.randint(part_keys[1], (SEQ_LEN,), 0, SEQ_LEN) < 5).astype(jnp.int32), jax.random.fold_in(part_keys[1], 1), 0, 1)
    cotangent = noise(part_keys[2], (SEQ_LEN, D), 0.01, 0.059814453, ((0, 4), (1, 2)))
    input_weight = noise(key_list[3], (D, INNER), D ** -0.5, 0.1875, ((0, 8), (1, 2)))
    gate_weight = noise(key_list[4], (D, INNER), D ** -0.5, 0.1875, ((0, 8), (1, 2)))
    key_weight = noise(key_list[5], (D, GROUPS * STATE), (8 * D) ** -0.5, 0.0625, ((0, 8), (1, 2)))
    query_weight = noise(key_list[6], (D, GROUPS * STATE), (8 * D) ** -0.5, 0.0625, ((0, 8), (1, 2)))
    step_weight = noise(key_list[7], (D, HEADS), D ** -0.5, 0.1875, ((0, 8), (1, 2)))
    output_weight = noise(key_list[8], (D, INNER), INNER ** -0.5, 0.125, ((0, 8), (1, 2)))
    step_bias = jnp.clip(-4.5 + 2.5 * jax.random.uniform(key_list[9], (HEADS,), jnp.float32) ** block_scale(key_list[9], (HEADS,), ((0, 2),), -0.2, 0.2), -4.5, -2.0)
    decay_log = draw_decay_log(jax.random.fold_in(key_list[12], 71), part)
    skip_gain = jnp.clip(0.5 + 1.5 * jax.random.uniform(key_list[11], (HEADS,), jnp.float32) ** block_scale(key_list[11], (HEADS,), ((0, 2),), -0.2, 0.2), 0.5, 2.0)
    return {"hidden": hidden, "breaks": breaks, "cotangent": cotangent, "input_weight": input_weight, "gate_weight": gate_weight, "key_weight": key_weight, "query_weight": query_weight, "step_weight": step_weight, "output_weight": output_weight, "step_bias": step_bias, "decay_log": decay_log, "skip_gain": skip_gain}


KEEP_LOG = -0.35667494393873245
EPSILON = 1e-05

def block_terms(step_bias, decay_log, break_marks, inner_vals, key_vals, query_vals, step_raw):
    length = inner_vals.shape[0]
    blocks = length // STRETCH
    head_count = inner_vals.shape[1]
    groups = key_vals.shape[1]
    per_group = head_count // groups
    step_size = jax.nn.softplus(step_raw + step_bias)
    log_rates = -jnp.exp(decay_log) * step_size + KEEP_LOG * break_marks[:, None]
    log_decay = jnp.cumsum(log_rates.reshape(blocks, STRETCH, head_count), axis=1)
    step_blocks = step_size.reshape(blocks, STRETCH, head_count)
    key_blocks = key_vals.reshape(blocks, STRETCH, groups, -1).astype(jnp.float32)
    query_blocks = query_vals.reshape(blocks, STRETCH, groups, -1).astype(jnp.float32)
    inner_blocks = inner_vals.reshape(blocks, STRETCH, groups, per_group, -1)
    scores = jnp.einsum('cqgn,ckgn->cgqk', query_blocks, key_blocks, precision=lax.Precision.HIGHEST)
    decay_rows = jnp.transpose(log_decay, (0, 2, 1)).reshape(blocks, groups, per_group, STRETCH)
    step_rows = jnp.transpose(step_blocks, (0, 2, 1)).reshape(blocks, groups, per_group, STRETCH)
    causal = lax.broadcasted_iota(jnp.int32, (STRETCH, STRETCH), 0) >= lax.broadcasted_iota(jnp.int32, (STRETCH, STRETCH), 1)
    spread = decay_rows[..., :, None] - decay_rows[..., None, :]
    within = jnp.where(causal, jnp.exp(jnp.where(causal, spread, 0.0)), 0.0)
    mixing = (scores[:, :, None] * within * step_rows[..., None, :]).astype(jnp.bfloat16)
    local_out = jnp.einsum('cghqk,ckghp->cqghp', mixing.astype(jnp.float32), inner_blocks.astype(jnp.float32), precision=lax.Precision.HIGHEST)
    to_end = (jnp.exp(log_decay[:, -1:, :] - log_decay) * step_blocks).reshape(blocks, STRETCH, groups, per_group)
    weighted = (inner_blocks * to_end[..., None]).astype(jnp.bfloat16)
    block_states = jnp.einsum('cqghp,cqgn->cghpn', weighted.astype(jnp.float32), key_blocks, precision=lax.Precision.HIGHEST)
    block_decay = jnp.exp(log_decay[:, -1, :]).reshape(blocks, groups, per_group)

    def advance(running, current):
        kept_decay, kept_state = running
        decay_now, state_now = current
        return ((kept_decay * decay_now, decay_now[..., None, None] * kept_state + state_now), (kept_decay, kept_state))
    initial = (jnp.ones(block_decay.shape[1:], jnp.float32), jnp.zeros(block_states.shape[1:], jnp.float32))
    totals, priors = lax.scan(advance, initial, (block_decay, block_states))
    return (local_out, priors[1], priors[0], log_decay, totals[0], totals[1])

def finish_terms(skip_gain, local_out, prior_state, prior_decay, log_decay, total_decay, total_state, query_vals, inner_vals, entering):
    blocks = log_decay.shape[0]
    groups = query_vals.shape[1]
    per_group = inner_vals.shape[1] // groups
    states = prior_state + prior_decay[..., None, None] * entering
    query_full = query_vals.reshape(blocks, STRETCH, groups, -1).astype(jnp.float32)
    carried = jnp.einsum('cqgn,cghpn->cqghp', query_full, states, precision=lax.Precision.HIGHEST)
    growth = jnp.exp(log_decay).reshape(blocks, STRETCH, groups, per_group)
    inner_full = inner_vals.reshape(blocks, STRETCH, groups, per_group, -1).astype(jnp.float32)
    mixer_out = local_out + growth[..., None] * carried + skip_gain.reshape(groups, per_group)[:, :, None] * inner_full
    leaving = total_decay[..., None, None] * entering + total_state
    return (mixer_out.reshape(blocks * STRETCH, groups, -1), leaving)

def gate_terms(mixer_out, gate_vals):
    product = mixer_out * jax.nn.silu(gate_vals.astype(jnp.float32))
    scaled = product * lax.rsqrt(lax.optimization_barrier(jnp.mean(product * product, axis=-1, keepdims=True)) + EPSILON)
    return scaled.astype(jnp.bfloat16)

def group_mixer(bias_part, log_part, skip_part, break_marks, inner_vals, gate_vals, key_vals, query_vals, step_raw):
    length = inner_vals.shape[0]
    inner_heads = inner_vals.reshape(length, -1, HEAD_DIM)
    key_heads = key_vals.reshape(length, 1, -1)
    query_heads = query_vals.reshape(length, 1, -1)
    local_terms = block_terms(bias_part, log_part, break_marks, inner_heads, key_heads, query_heads, step_raw)
    entering = jnp.zeros(local_terms[5].shape, jnp.float32)
    mixer_out, leaving = finish_terms(skip_part, *local_terms, query_heads, inner_heads, entering)
    return gate_terms(mixer_out, gate_vals.reshape(length, 1, -1)).reshape(length, -1)

def block_grad(left_side, right_side):
    block_count = left_side.shape[0] // TOK_DEV
    left_blocks = left_side.astype(jnp.float32).reshape(block_count, TOK_DEV, -1)
    right_blocks = right_side.astype(jnp.float32).reshape(block_count, TOK_DEV, -1)
    products = jnp.einsum('btd,btk->bdk', left_blocks, right_blocks, precision=lax.Precision.HIGHEST)
    rounded = lax.optimization_barrier(products.astype(jnp.bfloat16))
    return lax.optimization_barrier(jnp.sum(rounded.astype(jnp.float32), axis=0))

def reference(hidden, breaks, cotangent, input_weight, gate_weight, key_weight, query_weight, step_weight, output_weight, step_bias, decay_log, skip_gain):
    per_group = HEADS // GROUPS
    width_group = per_group * HEAD_DIM
    per_shard = GROUPS // N_MP
    all_marks = breaks.astype(jnp.float32)
    grad_input = jnp.zeros(input_weight.shape, jnp.float32)
    grad_gate = jnp.zeros(gate_weight.shape, jnp.float32)
    grad_key = jnp.zeros(key_weight.shape, jnp.float32)
    grad_query = jnp.zeros(query_weight.shape, jnp.float32)
    grad_step = jnp.zeros(step_weight.shape, jnp.float32)
    grad_output = jnp.zeros(output_weight.shape, jnp.float32)
    strand_totals = []
    for strand_index in range(2):
        if strand_index == 0:
            source = hidden
            break_marks = all_marks
            grads_in = cotangent
        else:
            source = jnp.flip(hidden, (0, 1))
            break_marks = jnp.flip(all_marks)
            grads_in = jnp.flip(cotangent, (0, 1))
        inner_all = jnp.dot(source, input_weight, preferred_element_type=jnp.float32).astype(jnp.bfloat16)
        gate_all = jnp.dot(source, gate_weight, preferred_element_type=jnp.float32).astype(jnp.bfloat16)
        key_all = jnp.dot(source, key_weight, preferred_element_type=jnp.float32).astype(jnp.bfloat16)
        query_all = jnp.dot(source, query_weight, preferred_element_type=jnp.float32).astype(jnp.bfloat16)
        step_all = jnp.dot(source, step_weight, preferred_element_type=jnp.float32)
        strand_total = jnp.zeros((SEQ_LEN, D), jnp.float32)
        shard_sum = jnp.zeros((SEQ_LEN, D), jnp.float32)
        for group_index in range(GROUPS):
            col_span = slice(group_index * width_group, (group_index + 1) * width_group)
            key_span = slice(group_index * STATE, (group_index + 1) * STATE)
            head_span = slice(group_index * per_group, (group_index + 1) * per_group)
            apply_group = partial(group_mixer, step_bias[head_span], decay_log[head_span], skip_gain[head_span], break_marks)
            gated, pullback = jax.vjp(apply_group, inner_all[:, col_span], gate_all[:, col_span], key_all[:, key_span], query_all[:, key_span], step_all[:, head_span])
            out_columns = output_weight[:, col_span]
            shard_sum = shard_sum + lax.dot_general(gated, out_columns, (((1,), (1,)), ((), ())), preferred_element_type=jnp.float32)
            if (group_index + 1) % per_shard == 0:
                strand_total = strand_total + lax.optimization_barrier(shard_sum.astype(jnp.bfloat16)).astype(jnp.float32)
                shard_sum = jnp.zeros((SEQ_LEN, D), jnp.float32)
            gated_back = jnp.dot(grads_in, out_columns, preferred_element_type=jnp.float32).astype(jnp.bfloat16)
            inner_back, gate_back, key_back, query_back, step_back = pullback(gated_back)
            grad_input = grad_input.at[:, col_span].add(block_grad(source, inner_back))
            grad_gate = grad_gate.at[:, col_span].add(block_grad(source, gate_back))
            grad_key = grad_key.at[:, key_span].add(block_grad(source, key_back))
            grad_query = grad_query.at[:, key_span].add(block_grad(source, query_back))
            grad_step = grad_step.at[:, head_span].add(block_grad(source, step_back))
            grad_output = grad_output.at[:, col_span].add(block_grad(grads_in, gated))
        strand_totals.append(strand_total)
    combined = (strand_totals[0] + jnp.flip(strand_totals[1], (0, 1))).astype(jnp.bfloat16)
    return (combined, grad_input, grad_gate, grad_key, grad_query, grad_step, grad_output)
```

```python
from functools import partial

import jax
import jax.numpy as jnp
from jax import lax
from jax.sharding import PartitionSpec as P

HEAD_DIM = 64
STATE = 128
STRETCH = 256


KEEP_LOG = -0.35667494393873245
EPSILON = 1e-05
HIGHEST = lax.Precision.HIGHEST


def swap(value, axis):
    size = lax.axis_size(axis)
    return lax.ppermute(value, axis, [(i, size - 1 - i) for i in range(size)])


def earlier_than(count, backward):
    row = lax.broadcasted_iota(jnp.int32, (count, count), 0)
    column = lax.broadcasted_iota(jnp.int32, (count, count), 1)
    return jnp.where(backward, column > row, column < row)


def chain_weights(before, logs):
    steps = before.astype(jnp.float32)
    between = steps[:, None, :] * jnp.transpose(steps)[None, :, :]
    spans = jnp.sum(between[..., None] * logs[None, None], axis=2)
    return jnp.where(before[..., None], jnp.exp(spans), 0.0)


def block_terms(
    backward, step_bias, decay_log, break_marks, inner_vals, key_vals, query_vals, step_raw
):
    length = inner_vals.shape[0]
    blocks = length // STRETCH
    head_count = inner_vals.shape[1]
    groups = key_vals.shape[1]
    per_group = head_count // groups
    before = earlier_than(STRETCH, backward)
    row = lax.broadcasted_iota(jnp.int32, (STRETCH, STRETCH), 0)
    column = lax.broadcasted_iota(jnp.int32, (STRETCH, STRETCH), 1)
    causal = before | (row == column)
    step_size = jax.nn.softplus(step_raw + step_bias)
    log_rates = -jnp.exp(decay_log) * step_size + KEEP_LOG * break_marks[:, None]
    rate_rows = jnp.transpose(log_rates.reshape(blocks, STRETCH, head_count), (0, 2, 1))
    step_rows = jnp.transpose(step_size.reshape(blocks, STRETCH, head_count), (0, 2, 1))
    log_rows = jnp.einsum("chj,ij->chi", rate_rows, causal.astype(jnp.float32), precision=HIGHEST)
    ends = jnp.sum(rate_rows, axis=-1)
    end_rows = jnp.exp(ends[..., None] - log_rows) * step_rows
    log_decay = jnp.transpose(log_rows, (0, 2, 1))
    key_blocks = key_vals.reshape(blocks, STRETCH, groups, -1)
    query_blocks = query_vals.reshape(blocks, STRETCH, groups, -1)
    inner_blocks = inner_vals.reshape(blocks, STRETCH, groups, per_group, -1)
    scores = jnp.einsum(
        "cqgn,ckgn->cgqk", query_blocks, key_blocks, preferred_element_type=jnp.float32
    )
    decay_rows = log_rows.reshape(blocks, groups, per_group, STRETCH)
    step_heads = step_rows.reshape(blocks, groups, per_group, STRETCH)
    spread = decay_rows[..., :, None] - decay_rows[..., None, :]
    within = jnp.where(causal, jnp.exp(jnp.where(causal, spread, 0.0)), 0.0)
    mixing = (scores[:, :, None] * within * step_heads[..., None, :]).astype(jnp.bfloat16)
    local_out = jnp.einsum(
        "cghqk,ckghp->cqghp", mixing, inner_blocks, preferred_element_type=jnp.float32
    )
    to_end = jnp.transpose(end_rows, (0, 2, 1)).reshape(blocks, STRETCH, groups, per_group)
    weighted = (inner_blocks * to_end[..., None]).astype(jnp.bfloat16)
    block_states = jnp.einsum(
        "cqghp,cqgn->cghpn", weighted, key_blocks, preferred_element_type=jnp.float32
    )
    order = earlier_than(blocks, backward)
    head_shape = (groups, per_group)
    weights = chain_weights(order, ends).reshape((blocks, blocks) + head_shape)
    prior_state = jnp.stack(
        [
            sum(
                weights[c, k][..., None, None] * block_states[k] for k in range(blocks) if k != c
            )
            if blocks > 1
            else jnp.zeros_like(block_states[0])
            for c in range(blocks)
        ]
    )
    order_f = order.astype(jnp.float32)
    prior_logs = jnp.sum(order_f[:, :, None] * ends[None], axis=1)
    later_logs = jnp.sum(jnp.transpose(order_f)[:, :, None] * ends[None], axis=1)
    prior_decay = jnp.exp(prior_logs).reshape((blocks,) + head_shape)
    later_decay = jnp.exp(later_logs).reshape((blocks,) + head_shape)
    total_state = sum(later_decay[c][..., None, None] * block_states[c] for c in range(blocks))
    total_log = jnp.sum(ends, axis=0)
    return (local_out, prior_state, prior_decay, log_decay, total_log, total_state)


def finish_terms(
    skip_gain,
    local_out,
    prior_state,
    prior_decay,
    log_decay,
    query_vals,
    inner_vals,
    entering,
):
    blocks = log_decay.shape[0]
    groups = query_vals.shape[1]
    per_group = inner_vals.shape[1] // groups
    states = prior_state + prior_decay[..., None, None] * entering
    query_full = query_vals.reshape(blocks, STRETCH, groups, -1).astype(jnp.float32)
    carried = jnp.einsum("cqgn,cghpn->cqghp", query_full, states, precision=HIGHEST)
    growth = jnp.exp(log_decay).reshape(blocks, STRETCH, groups, per_group)
    inner_full = inner_vals.reshape(blocks, STRETCH, groups, per_group, -1).astype(jnp.float32)
    mixer_out = (
        local_out
        + growth[..., None] * carried
        + skip_gain.reshape(groups, per_group)[:, :, None] * inner_full
    )
    return mixer_out.reshape(blocks * STRETCH, groups, -1)


def gate_terms(mixer_out, gate_vals):
    product = mixer_out * jax.nn.silu(gate_vals.astype(jnp.float32))
    scaled = product * lax.rsqrt(jnp.mean(product * product, axis=-1, keepdims=True) + EPSILON)
    return scaled.astype(jnp.bfloat16)


def gather_pair(shard):
    own = lax.all_gather(shard, "seq", axis=0, tiled=True)
    return (own, swap(own, "strand"))


def pair_dot(left, right):
    return jnp.dot(left[0], right[0], preferred_element_type=jnp.float32) + jnp.dot(
        left[1], right[1], preferred_element_type=jnp.float32
    )


def share_sum(own, other):
    arrived = swap(other, "strand")
    both = (own.astype(jnp.float32) + arrived.astype(jnp.float32)).astype(jnp.bfloat16)
    return lax.psum_scatter(both, "seq", scatter_dimension=0, tiled=True)


def on_device(
    hidden,
    breaks,
    cotangent,
    input_weight,
    gate_weight,
    key_weight,
    query_weight,
    step_weight,
    output_weight,
    step_bias,
    decay_log,
    skip_gain,
):
    strand = lax.axis_index("strand")
    backward = strand == 1
    seq_index = lax.axis_index("seq")
    length = hidden.shape[0]
    shard_rows = input_weight.shape[0]
    peers = lax.axis_size("seq")
    halves = lax.axis_size("mp")
    width = shard_rows * peers * 2
    half = shard_rows * peers
    part_width = hidden.shape[1]

    target = lax.broadcasted_iota(jnp.int32, (width, width), 1)
    source = lax.broadcasted_iota(jnp.int32, (width, width), 0)
    local = target % half
    side = jnp.where(target < half, strand, 1 - strand)
    feature = (local // shard_rows) * (2 * shard_rows) + side * shard_rows + local % shard_rows
    feature = jnp.where(backward, width - 1 - feature, feature)
    moves = (source == feature).astype(jnp.bfloat16)
    moves = lax.optimization_barrier(moves)

    def permuted(everything):
        total = sum(
            jnp.dot(
                everything[m],
                moves[m * part_width : (m + 1) * part_width],
                preferred_element_type=jnp.float32,
            )
            for m in range(halves)
        ).astype(jnp.bfloat16)
        return (total[:, :half], total[:, half:])

    inputs = permuted(lax.all_gather(hidden, "mp", axis=0))
    grads_in = permuted(lax.all_gather(cotangent, "mp", axis=0))
    break_marks = lax.dynamic_slice_in_dim(breaks, seq_index * length, length).astype(jnp.float32)

    key_width = key_weight.shape[1]
    small = jnp.concatenate((key_weight, query_weight, step_weight), axis=1)
    small_full = gather_pair(small)
    inner_full = gather_pair(input_weight)
    gate_full = gather_pair(gate_weight)
    out_full = gather_pair(output_weight)

    small_out = pair_dot(inputs, small_full)
    groups = key_width // STATE
    key_vals = small_out[:, :key_width].astype(jnp.bfloat16).reshape(length, groups, STATE)
    query_vals = (
        small_out[:, key_width : 2 * key_width].astype(jnp.bfloat16).reshape(length, groups, STATE)
    )
    step_raw = small_out[:, 2 * key_width :]
    inner_vals = pair_dot(inputs, inner_full).astype(jnp.bfloat16).reshape(length, -1, HEAD_DIM)
    gate_vals = pair_dot(inputs, gate_full).astype(jnp.bfloat16).reshape(length, groups, -1)

    local_terms, local_pull = jax.vjp(
        partial(block_terms, backward, step_bias, decay_log, break_marks),
        inner_vals,
        key_vals,
        query_vals,
        step_raw,
    )
    total_log, total_state = local_terms[4:]
    head_shape = total_state.shape[:2]
    all_logs = lax.all_gather(total_log, "seq")
    order = earlier_than(peers, backward)
    chain = chain_weights(order, all_logs)
    here = lax.dynamic_index_in_dim(chain, seq_index, 0, keepdims=False)
    there = lax.dynamic_index_in_dim(chain, seq_index, 1, keepdims=False)

    def chained(value, weights):
        everything = lax.all_gather(value.astype(jnp.bfloat16), "seq")
        weights = weights.reshape((peers,) + head_shape)
        return sum(
            weights[k][..., None, None] * everything[k].astype(jnp.float32) for k in range(peers)
        )

    entering = chained(total_state, here)
    mixer_out, finish_pull = jax.vjp(
        partial(finish_terms, skip_gain), *local_terms[:4], query_vals, inner_vals, entering
    )
    gated, gate_pull = jax.vjp(gate_terms, mixer_out, gate_vals)
    gated_flat = gated.reshape(length, -1)

    gated_back = pair_dot(grads_in, out_full).astype(jnp.bfloat16).reshape(gated.shape)
    mixer_back, gate_back = gate_pull(gated_back)
    finish_back = finish_pull(mixer_back)
    carried_back = chained(finish_back[6], there)

    contract_rows = (((1,), (1,)), ((), ()))
    head_terms = tuple(
        lax.dot_general(
            gated_flat, part, contract_rows, preferred_element_type=jnp.float32
        ).astype(jnp.bfloat16)
        for part in out_full
    )
    head_terms = jnp.stack(
        [
            sum(
                lax.dot_general(
                    head_terms[s],
                    moves[m * part_width : (m + 1) * part_width, s * half : (s + 1) * half],
                    contract_rows,
                    preferred_element_type=jnp.float32,
                )
                for s in range(2)
            ).astype(jnp.bfloat16)
            for m in range(halves)
        ]
    )
    reduced = lax.psum_scatter(head_terms, "mp", scatter_dimension=0)
    combined = (
        reduced.astype(jnp.float32) + swap(reduced, "strand").astype(jnp.float32)
    ).astype(jnp.bfloat16)

    contract = (((0,), (0,)), ((), ()))

    def shared_grad(left, right):
        own, other = (
            lax.dot_general(part, right, contract, preferred_element_type=jnp.float32).astype(
                jnp.bfloat16
            )
            for part in left
        )
        return share_sum(own, other).astype(jnp.float32)

    grad_output = shared_grad(grads_in, gated_flat)
    grad_gate = shared_grad(inputs, gate_back.reshape(length, -1))

    log_back = jnp.sum(carried_back * entering, axis=(-2, -1)).reshape(
        total_log.shape
    ) * jnp.exp(total_log)
    local_back = local_pull((*finish_back[:4], log_back, carried_back))
    inner_back = (local_back[0] + finish_back[5]).reshape(length, -1)
    key_back = local_back[1].reshape(length, -1)
    query_back = (local_back[2] + finish_back[4]).reshape(length, -1)
    step_back = local_back[3]

    grad_input = shared_grad(inputs, inner_back)
    small_terms = tuple(
        jnp.concatenate(
            (
                lax.dot_general(
                    part, key_back, contract, preferred_element_type=jnp.float32
                ).astype(jnp.bfloat16),
                lax.dot_general(
                    part, query_back, contract, preferred_element_type=jnp.float32
                ).astype(jnp.bfloat16),
                lax.dot_general(
                    part.astype(jnp.float32), step_back, contract, precision=HIGHEST
                ).astype(jnp.bfloat16),
            ),
            axis=1,
        )
        for part in inputs
    )
    small_share = share_sum(*small_terms).astype(jnp.float32)
    return (
        combined,
        grad_input,
        grad_gate,
        small_share[:, :key_width],
        small_share[:, key_width : 2 * key_width],
        small_share[:, 2 * key_width :],
        grad_output,
    )


def solution(mesh):
    in_specs = (
        P(("parts", "seq"), "mp"),
        P("parts"),
        P(("parts", "seq"), "mp"),
        P(("seq", "strand"), "mp"),
        P(("seq", "strand"), "mp"),
        P(("seq", "strand"), "mp"),
        P(("seq", "strand"), "mp"),
        P(("seq", "strand"), "mp"),
        P(("seq", "strand"), "mp"),
        P("mp"),
        P("mp"),
        P("mp"),
    )
    out_specs = (
        P(("parts", "seq"), "mp"),
        P(("parts", "seq", "strand"), "mp"),
        P(("parts", "seq", "strand"), "mp"),
        P(("parts", "seq", "strand"), "mp"),
        P(("parts", "seq", "strand"), "mp"),
        P(("parts", "seq", "strand"), "mp"),
        P(("parts", "seq", "strand"), "mp"),
    )
    return jax.shard_map(
        on_device, mesh=mesh, in_specs=in_specs, out_specs=out_specs, check_vma=False
    )
```

```python
from functools import partial

import jax
import jax.numpy as jnp
from jax import lax
from jax.experimental import pallas as pl
from jax.experimental.pallas import tpu as pltpu
from jax.sharding import PartitionSpec as P

HEAD_DIM = 64
STATE = 128
STRETCH = 256


KEEP_LOG = -0.35667494393873245
EPSILON = 1e-05
HIGHEST = lax.Precision.HIGHEST


def swap(value, axis):
    size = lax.axis_size(axis)
    return lax.ppermute(value, axis, [(i, size - 1 - i) for i in range(size)])


def earlier_than(count, backward):
    row = lax.broadcasted_iota(jnp.int32, (count, count), 0)
    column = lax.broadcasted_iota(jnp.int32, (count, count), 1)
    return jnp.where(backward, column > row, column < row)


def chain_weights(before, logs):
    steps = before.astype(jnp.float32)
    between = steps[:, None, :] * jnp.transpose(steps)[None, :, :]
    spans = jnp.sum(between[..., None] * logs[None, None], axis=2)
    return jnp.where(before[..., None], jnp.exp(spans), 0.0)


def block_terms(
    backward, step_bias, decay_log, break_marks, inner_vals, key_vals, query_vals, step_raw
):
    length = inner_vals.shape[0]
    blocks = length // STRETCH
    head_count = inner_vals.shape[1]
    groups = key_vals.shape[1]
    per_group = head_count // groups
    before = earlier_than(STRETCH, backward)
    row = lax.broadcasted_iota(jnp.int32, (STRETCH, STRETCH), 0)
    column = lax.broadcasted_iota(jnp.int32, (STRETCH, STRETCH), 1)
    causal = before | (row == column)
    step_size = jax.nn.softplus(step_raw + step_bias)
    log_rates = -jnp.exp(decay_log) * step_size + KEEP_LOG * break_marks[:, None]
    rate_rows = jnp.transpose(log_rates.reshape(blocks, STRETCH, head_count), (0, 2, 1))
    step_rows = jnp.transpose(step_size.reshape(blocks, STRETCH, head_count), (0, 2, 1))
    log_rows = jnp.einsum("chj,ij->chi", rate_rows, causal.astype(jnp.float32), precision=HIGHEST)
    ends = jnp.sum(rate_rows, axis=-1)
    end_rows = jnp.exp(ends[..., None] - log_rows) * step_rows
    log_decay = jnp.transpose(log_rows, (0, 2, 1))
    key_blocks = key_vals.reshape(blocks, STRETCH, groups, -1)
    query_blocks = query_vals.reshape(blocks, STRETCH, groups, -1)
    inner_blocks = inner_vals.reshape(blocks, STRETCH, groups, per_group, -1)
    scores = jnp.einsum(
        "cqgn,ckgn->cgqk", query_blocks, key_blocks, preferred_element_type=jnp.float32
    )
    decay_rows = log_rows.reshape(blocks, groups, per_group, STRETCH)
    step_heads = step_rows.reshape(blocks, groups, per_group, STRETCH)
    spread = decay_rows[..., :, None] - decay_rows[..., None, :]
    within = jnp.where(causal, jnp.exp(jnp.where(causal, spread, 0.0)), 0.0)
    mixing = (scores[:, :, None] * within * step_heads[..., None, :]).astype(jnp.bfloat16)
    local_out = jnp.einsum(
        "cghqk,ckghp->cqghp", mixing, inner_blocks, preferred_element_type=jnp.float32
    )
    to_end = jnp.transpose(end_rows, (0, 2, 1)).reshape(blocks, STRETCH, groups, per_group)
    weighted = (inner_blocks * to_end[..., None]).astype(jnp.bfloat16)
    block_states = jnp.einsum(
        "cqghp,cqgn->cghpn", weighted, key_blocks, preferred_element_type=jnp.float32
    )
    order = earlier_than(blocks, backward)
    head_shape = (groups, per_group)
    weights = chain_weights(order, ends).reshape((blocks, blocks) + head_shape)
    prior_state = jnp.stack(
        [
            sum(
                weights[c, k][..., None, None] * block_states[k] for k in range(blocks) if k != c
            )
            if blocks > 1
            else jnp.zeros_like(block_states[0])
            for c in range(blocks)
        ]
    )
    order_f = order.astype(jnp.float32)
    prior_logs = jnp.sum(order_f[:, :, None] * ends[None], axis=1)
    later_logs = jnp.sum(jnp.transpose(order_f)[:, :, None] * ends[None], axis=1)
    prior_decay = jnp.exp(prior_logs).reshape((blocks,) + head_shape)
    later_decay = jnp.exp(later_logs).reshape((blocks,) + head_shape)
    total_state = sum(later_decay[c][..., None, None] * block_states[c] for c in range(blocks))
    total_log = jnp.sum(ends, axis=0)
    return (local_out, prior_state, prior_decay, log_decay, total_log, total_state)


def finish_terms(
    skip_gain,
    local_out,
    prior_state,
    prior_decay,
    log_decay,
    query_vals,
    inner_vals,
    entering,
):
    blocks = log_decay.shape[0]
    groups = query_vals.shape[1]
    per_group = inner_vals.shape[1] // groups
    states = prior_state + prior_decay[..., None, None] * entering
    query_full = query_vals.reshape(blocks, STRETCH, groups, -1).astype(jnp.float32)
    carried = jnp.einsum("cqgn,cghpn->cqghp", query_full, states, precision=HIGHEST)
    growth = jnp.exp(log_decay).reshape(blocks, STRETCH, groups, per_group)
    inner_full = inner_vals.reshape(blocks, STRETCH, groups, per_group, -1).astype(jnp.float32)
    mixer_out = (
        local_out
        + growth[..., None] * carried
        + skip_gain.reshape(groups, per_group)[:, :, None] * inner_full
    )
    return mixer_out.reshape(blocks * STRETCH, groups, -1)


def gate_terms(mixer_out, gate_vals):
    product = mixer_out * jax.nn.silu(gate_vals.astype(jnp.float32))
    scaled = product * lax.rsqrt(jnp.mean(product * product, axis=-1, keepdims=True) + EPSILON)
    return scaled.astype(jnp.bfloat16)


def gather_kernel(peers, halves, *refs):
    shards, rows, fulls, all_rows = refs[:2], refs[2], refs[3:5], refs[5]
    local_sem, z_send, z_recv, y_send, y_recv, s_send, s_recv, o_send, o_recv, x_send, x_recv = refs[6:]
    part = lax.axis_index("parts")
    seq = lax.axis_index("seq")
    strand = lax.axis_index("strand")
    model = lax.axis_index("mp")
    twin = {"parts": 1 - part}
    mate = {"strand": 1 - strand}
    others = [lax.rem(seq + d, peers) for d in range(1, peers)]
    models = [lax.rem(model + d, halves) for d in range(1, halves)]

    def remote(source, target, send, receive, device):
        return pltpu.make_async_remote_copy(
            src_ref=source,
            dst_ref=target,
            send_sem=send,
            recv_sem=receive,
            device_id=device,
            device_id_type=pl.DeviceIdType.MESH,
        )

    barrier = pltpu.get_barrier_semaphore()
    targets = [{"seq": t} for t in others] + [{"mp": m} for m in models] + [twin, mate]
    for target in targets:
        pl.semaphore_signal(
            barrier, inc=1, device_id=target, device_id_type=pl.DeviceIdType.MESH
        )
    pl.semaphore_wait(barrier, len(targets))

    sends = []
    locals_ = []

    def go(copy):
        copy.start()
        sends.append(copy)

    for w in range(2):
        for d, t in enumerate(others):
            go(
                remote(
                    shards[w].at[part],
                    fulls[w].at[0, seq, part],
                    z_send.at[w, d],
                    z_recv.at[w, seq],
                    {"seq": t},
                )
            )
    for d, m in enumerate(models):
        go(remote(rows, all_rows.at[model], x_send.at[d], x_recv.at[model], {"mp": m}))
    for w in range(2):
        go(remote(shards[w], fulls[w].at[1, seq], o_send.at[w], o_recv.at[w], mate))
        copy = pltpu.make_async_copy(shards[w], fulls[w].at[0, seq], local_sem.at[w])
        copy.start()
        locals_.append(copy)
    copy = pltpu.make_async_copy(rows, all_rows.at[model], local_sem.at[2])
    copy.start()
    locals_.append(copy)

    for w in range(2):
        full = fulls[w]
        for d, t in enumerate(others):
            mine = full.at[0, t, part]
            remote(mine, mine, z_send.at[w, d], z_recv.at[w, t], {"seq": t}).wait_recv()
            go(remote(mine, mine, y_send.at[w, d], y_recv.at[w, t], twin))
            go(remote(mine, full.at[1, t, part], s_send.at[w, d, 0], s_recv.at[w, t, part], mate))
    for w in range(2):
        full = fulls[w]
        for d, t in enumerate(others):
            theirs = full.at[0, t, 1 - part]
            remote(theirs, theirs, y_send.at[w, d], y_recv.at[w, t], twin).wait_recv()
            go(
                remote(
                    theirs,
                    full.at[1, t, 1 - part],
                    s_send.at[w, d, 1],
                    s_recv.at[w, t, 1 - part],
                    mate,
                )
            )
    for w in range(2):
        full = fulls[w]
        own = full.at[1, seq]
        remote(own, own, o_send.at[w], o_recv.at[w], mate).wait_recv()
        for d, t in enumerate(others):
            for h in range(2):
                block = full.at[1, t, h]
                remote(block, block, s_send.at[w, d, h], s_recv.at[w, t, h], mate).wait_recv()
    for d, m in enumerate(models):
        block = all_rows.at[m]
        remote(block, block, x_send.at[d], x_recv.at[m], {"mp": m}).wait_recv()
    for copy in sends:
        copy.wait_send()
    for copy in locals_:
        copy.wait()


def gather_all(first, second, rows):
    peers, halves = (lax.axis_size("seq"), lax.axis_size("mp"))
    depth = first.shape[0] // 2
    shards = tuple(a.reshape(2, depth, -1) for a in (first, second))
    anywhere = pl.BlockSpec(memory_space=pl.ANY)
    dma = pltpu.SemaphoreType.DMA
    out = pl.pallas_call(
        partial(gather_kernel, peers, halves),
        out_shape=tuple(
            jax.ShapeDtypeStruct((2, peers) + a.shape, a.dtype) for a in shards
        )
        + (jax.ShapeDtypeStruct((halves,) + rows.shape, rows.dtype),),
        in_specs=[anywhere] * 3,
        out_specs=(anywhere,) * 3,
        scratch_shapes=[
            dma((3,)),
            dma((2, peers)),
            dma((2, peers)),
            dma((2, peers)),
            dma((2, peers)),
            dma((2, peers, 2)),
            dma((2, peers, 2)),
            dma((2,)),
            dma((2,)),
            dma((halves,)),
            dma((halves,)),
        ],
        compiler_params=pltpu.CompilerParams(collective_id=0, has_side_effects=True),
    )(*shards, rows)
    return (
        out[0].reshape(4 * peers * depth, -1),
        out[1].reshape(4 * peers * depth, -1),
        out[2],
    )


def share_sum(own, other):
    arrived = swap(other, "strand")
    both = (own.astype(jnp.float32) + arrived.astype(jnp.float32)).astype(jnp.bfloat16)
    return lax.psum_scatter(both, "seq", scatter_dimension=0, tiled=True)


def on_device(
    hidden,
    breaks,
    cotangent,
    input_weight,
    gate_weight,
    key_weight,
    query_weight,
    step_weight,
    output_weight,
    step_bias,
    decay_log,
    skip_gain,
):
    strand = lax.axis_index("strand")
    backward = strand == 1
    seq_index = lax.axis_index("seq")
    length = hidden.shape[0]
    shard_rows = input_weight.shape[0]
    peers = lax.axis_size("seq")
    halves = lax.axis_size("mp")
    width = shard_rows * peers * 2
    half = shard_rows * peers
    part_width = hidden.shape[1]

    target = lax.broadcasted_iota(jnp.int32, (width, width), 1)
    source = lax.broadcasted_iota(jnp.int32, (width, width), 0)
    local = target % half
    side = jnp.where(target < half, strand, 1 - strand)
    feature = (local // shard_rows) * (2 * shard_rows) + side * shard_rows + local % shard_rows
    feature = jnp.where(backward, width - 1 - feature, feature)
    moves = (source == feature).astype(jnp.bfloat16)
    moves = lax.optimization_barrier(moves)

    key_width = key_weight.shape[1]
    inner_width = input_weight.shape[1]
    ahead = jnp.concatenate(
        (input_weight, gate_weight, key_weight, query_weight, step_weight), axis=1
    )
    ahead_full, out_full, everything = gather_all(
        ahead, output_weight, jnp.stack((hidden, cotangent))
    )

    def permuted(which):
        return sum(
            jnp.dot(
                everything[m, which],
                moves[m * part_width : (m + 1) * part_width],
                preferred_element_type=jnp.float32,
            )
            for m in range(halves)
        ).astype(jnp.bfloat16)

    inputs = permuted(0)
    grads_in = permuted(1)
    break_marks = lax.dynamic_slice_in_dim(breaks, seq_index * length, length).astype(jnp.float32)

    def project(start, size):
        return jnp.dot(
            inputs, ahead_full[:, start : start + size], preferred_element_type=jnp.float32
        )

    groups = key_width // STATE
    key_start = 2 * inner_width
    key_vals = project(key_start, key_width).astype(jnp.bfloat16).reshape(length, groups, STATE)
    query_vals = (
        project(key_start + key_width, key_width)
        .astype(jnp.bfloat16)
        .reshape(length, groups, STATE)
    )
    step_raw = project(key_start + 2 * key_width, step_weight.shape[1])
    inner_vals = project(0, inner_width).astype(jnp.bfloat16).reshape(length, -1, HEAD_DIM)
    gate_vals = project(inner_width, inner_width).astype(jnp.bfloat16).reshape(length, groups, -1)

    local_terms, local_pull = jax.vjp(
        partial(block_terms, backward, step_bias, decay_log, break_marks),
        inner_vals,
        key_vals,
        query_vals,
        step_raw,
    )
    total_log, total_state = local_terms[4:]
    head_shape = total_state.shape[:2]
    all_logs = lax.all_gather(total_log, "seq")
    order = earlier_than(peers, backward)
    chain = chain_weights(order, all_logs)
    here = lax.dynamic_index_in_dim(chain, seq_index, 0, keepdims=False)
    there = lax.dynamic_index_in_dim(chain, seq_index, 1, keepdims=False)

    def chained(value, weights):
        everything = lax.all_gather(value.astype(jnp.bfloat16), "seq")
        weights = weights.reshape((peers,) + head_shape)
        return sum(
            weights[k][..., None, None] * everything[k].astype(jnp.float32) for k in range(peers)
        )

    entering = chained(total_state, here)
    mixer_out, finish_pull = jax.vjp(
        partial(finish_terms, skip_gain), *local_terms[:4], query_vals, inner_vals, entering
    )
    gated, gate_pull = jax.vjp(gate_terms, mixer_out, gate_vals)
    gated_flat = gated.reshape(length, -1)

    gated_back = jnp.dot(grads_in, out_full, preferred_element_type=jnp.float32).astype(jnp.bfloat16).reshape(gated.shape)
    mixer_back, gate_back = gate_pull(gated_back)
    finish_back = finish_pull(mixer_back)
    carried_back = chained(finish_back[6], there)

    contract_rows = (((1,), (1,)), ((), ()))
    head_terms = tuple(
        lax.dot_general(
            gated_flat, part, contract_rows, preferred_element_type=jnp.float32
        ).astype(jnp.bfloat16)
        for part in (out_full[:half], out_full[half:])
    )
    head_terms = jnp.stack(
        [
            sum(
                lax.dot_general(
                    head_terms[s],
                    moves[m * part_width : (m + 1) * part_width, s * half : (s + 1) * half],
                    contract_rows,
                    preferred_element_type=jnp.float32,
                )
                for s in range(2)
            ).astype(jnp.bfloat16)
            for m in range(halves)
        ]
    )
    reduced = lax.psum_scatter(head_terms, "mp", scatter_dimension=0)
    combined = (
        reduced.astype(jnp.float32) + swap(reduced, "strand").astype(jnp.float32)
    ).astype(jnp.bfloat16)

    contract = (((0,), (0,)), ((), ()))

    def shared_grad(left, right):
        own, other = (
            lax.dot_general(part, right, contract, preferred_element_type=jnp.float32).astype(
                jnp.bfloat16
            )
            for part in (left[:, :half], left[:, half:])
        )
        return share_sum(own, other).astype(jnp.float32)

    grad_output = shared_grad(grads_in, gated_flat)
    grad_gate = shared_grad(inputs, gate_back.reshape(length, -1))

    log_back = jnp.sum(carried_back * entering, axis=(-2, -1)).reshape(
        total_log.shape
    ) * jnp.exp(total_log)
    local_back = local_pull((*finish_back[:4], log_back, carried_back))
    inner_back = (local_back[0] + finish_back[5]).reshape(length, -1)
    key_back = local_back[1].reshape(length, -1)
    query_back = (local_back[2] + finish_back[4]).reshape(length, -1)
    step_back = local_back[3]

    grad_input = shared_grad(inputs, inner_back)
    small_terms = tuple(
        jnp.concatenate(
            (
                lax.dot_general(
                    part, key_back, contract, preferred_element_type=jnp.float32
                ).astype(jnp.bfloat16),
                lax.dot_general(
                    part, query_back, contract, preferred_element_type=jnp.float32
                ).astype(jnp.bfloat16),
                lax.dot_general(
                    part.astype(jnp.float32), step_back, contract, precision=HIGHEST
                ).astype(jnp.bfloat16),
            ),
            axis=1,
        )
        for part in (inputs[:, :half], inputs[:, half:])
    )
    small_share = share_sum(*small_terms).astype(jnp.float32)
    return (
        combined,
        grad_input,
        grad_gate,
        small_share[:, :key_width],
        small_share[:, key_width : 2 * key_width],
        small_share[:, 2 * key_width :],
        grad_output,
    )


def solution(mesh):
    in_specs = (
        P(("parts", "seq"), "mp"),
        P("parts"),
        P(("parts", "seq"), "mp"),
        P(("seq", "strand"), "mp"),
        P(("seq", "strand"), "mp"),
        P(("seq", "strand"), "mp"),
        P(("seq", "strand"), "mp"),
        P(("seq", "strand"), "mp"),
        P(("seq", "strand"), "mp"),
        P("mp"),
        P("mp"),
        P("mp"),
    )
    out_specs = (
        P(("parts", "seq"), "mp"),
        P(("parts", "seq", "strand"), "mp"),
        P(("parts", "seq", "strand"), "mp"),
        P(("parts", "seq", "strand"), "mp"),
        P(("parts", "seq", "strand"), "mp"),
        P(("parts", "seq", "strand"), "mp"),
        P(("parts", "seq", "strand"), "mp"),
    )
    return jax.shard_map(
        on_device, mesh=mesh, in_specs=in_specs, out_specs=out_specs, check_vma=False
    )
```

```python
from functools import partial

import jax
import jax.numpy as jnp
from jax import lax
from jax.experimental import pallas as pl
from jax.experimental.pallas import tpu as pltpu
from jax.sharding import PartitionSpec as P

HEAD_DIM = 64
STATE = 128
STRETCH = 256


KEEP_LOG = -0.35667494393873245
EPSILON = 1e-05
HIGHEST = lax.Precision.HIGHEST


def swap(value, axis):
    size = lax.axis_size(axis)
    return lax.ppermute(value, axis, [(i, size - 1 - i) for i in range(size)])


def earlier_than(count, backward):
    row = lax.broadcasted_iota(jnp.int32, (count, count), 0)
    column = lax.broadcasted_iota(jnp.int32, (count, count), 1)
    return jnp.where(backward, column > row, column < row)


def chain_weights(before, logs):
    steps = before.astype(jnp.float32)
    between = steps[:, None, :] * jnp.transpose(steps)[None, :, :]
    spans = jnp.sum(between[..., None] * logs[None, None], axis=2)
    return jnp.where(before[..., None], jnp.exp(spans), 0.0)


def block_terms(
    backward, step_bias, decay_log, break_marks, inner_vals, key_vals, query_vals, step_raw
):
    length = inner_vals.shape[0]
    blocks = length // STRETCH
    head_count = inner_vals.shape[1]
    groups = key_vals.shape[1]
    per_group = head_count // groups
    before = earlier_than(STRETCH, backward)
    row = lax.broadcasted_iota(jnp.int32, (STRETCH, STRETCH), 0)
    column = lax.broadcasted_iota(jnp.int32, (STRETCH, STRETCH), 1)
    causal = before | (row == column)
    step_size = jax.nn.softplus(step_raw + step_bias)
    log_rates = -jnp.exp(decay_log) * step_size + KEEP_LOG * break_marks[:, None]
    rate_rows = jnp.transpose(log_rates.reshape(blocks, STRETCH, head_count), (0, 2, 1))
    step_rows = jnp.transpose(step_size.reshape(blocks, STRETCH, head_count), (0, 2, 1))
    log_rows = jnp.einsum("chj,ij->chi", rate_rows, causal.astype(jnp.float32), precision=HIGHEST)
    ends = jnp.sum(rate_rows, axis=-1)
    end_rows = jnp.exp(ends[..., None] - log_rows) * step_rows
    log_decay = jnp.transpose(log_rows, (0, 2, 1))
    key_blocks = key_vals.reshape(blocks, STRETCH, groups, -1)
    query_blocks = query_vals.reshape(blocks, STRETCH, groups, -1)
    inner_blocks = inner_vals.reshape(blocks, STRETCH, groups, per_group, -1)
    scores = jnp.einsum(
        "cqgn,ckgn->cgqk", query_blocks, key_blocks, preferred_element_type=jnp.float32
    )
    decay_rows = log_rows.reshape(blocks, groups, per_group, STRETCH)
    step_heads = step_rows.reshape(blocks, groups, per_group, STRETCH)
    spread = decay_rows[..., :, None] - decay_rows[..., None, :]
    within = jnp.where(causal, jnp.exp(jnp.where(causal, spread, 0.0)), 0.0)
    mixing = (scores[:, :, None] * within * step_heads[..., None, :]).astype(jnp.bfloat16)
    local_out = jnp.einsum(
        "cghqk,ckghp->cqghp", mixing, inner_blocks, preferred_element_type=jnp.float32
    )
    to_end = jnp.transpose(end_rows, (0, 2, 1)).reshape(blocks, STRETCH, groups, per_group)
    weighted = (inner_blocks * to_end[..., None]).astype(jnp.bfloat16)
    block_states = jnp.einsum(
        "cqghp,cqgn->cghpn", weighted, key_blocks, preferred_element_type=jnp.float32
    )
    order = earlier_than(blocks, backward)
    head_shape = (groups, per_group)
    weights = chain_weights(order, ends).reshape((blocks, blocks) + head_shape)
    prior_state = jnp.stack(
        [
            sum(
                weights[c, k][..., None, None] * block_states[k] for k in range(blocks) if k != c
            )
            if blocks > 1
            else jnp.zeros_like(block_states[0])
            for c in range(blocks)
        ]
    )
    order_f = order.astype(jnp.float32)
    prior_logs = jnp.sum(order_f[:, :, None] * ends[None], axis=1)
    later_logs = jnp.sum(jnp.transpose(order_f)[:, :, None] * ends[None], axis=1)
    prior_decay = jnp.exp(prior_logs).reshape((blocks,) + head_shape)
    later_decay = jnp.exp(later_logs).reshape((blocks,) + head_shape)
    total_state = sum(later_decay[c][..., None, None] * block_states[c] for c in range(blocks))
    total_log = jnp.sum(ends, axis=0)
    return (local_out, prior_state, prior_decay, log_decay, total_log, total_state)


def finish_terms(
    skip_gain,
    local_out,
    prior_state,
    prior_decay,
    log_decay,
    query_vals,
    inner_vals,
    entering,
):
    blocks = log_decay.shape[0]
    groups = query_vals.shape[1]
    per_group = inner_vals.shape[1] // groups
    states = prior_state + prior_decay[..., None, None] * entering
    query_full = query_vals.reshape(blocks, STRETCH, groups, -1).astype(jnp.float32)
    carried = jnp.einsum("cqgn,cghpn->cqghp", query_full, states, precision=HIGHEST)
    growth = jnp.exp(log_decay).reshape(blocks, STRETCH, groups, per_group)
    inner_full = inner_vals.reshape(blocks, STRETCH, groups, per_group, -1).astype(jnp.float32)
    mixer_out = (
        local_out
        + growth[..., None] * carried
        + skip_gain.reshape(groups, per_group)[:, :, None] * inner_full
    )
    return mixer_out.reshape(blocks * STRETCH, groups, -1)


def gate_terms(mixer_out, gate_vals):
    product = mixer_out * jax.nn.silu(gate_vals.astype(jnp.float32))
    scaled = product * lax.rsqrt(jnp.mean(product * product, axis=-1, keepdims=True) + EPSILON)
    return scaled.astype(jnp.bfloat16)


def gather_kernel(peers, halves, *refs):
    shards, rows, fulls, all_rows = refs[:2], refs[2], refs[3:5], refs[5]
    local_sem, z_send, z_recv, y_send, y_recv, s_send, s_recv, o_send, o_recv, x_send, x_recv = refs[6:]
    part = lax.axis_index("parts")
    seq = lax.axis_index("seq")
    strand = lax.axis_index("strand")
    model = lax.axis_index("mp")
    twin = {"parts": 1 - part}
    mate = {"strand": 1 - strand}
    others = [lax.rem(seq + d, peers) for d in range(1, peers)]
    models = [lax.rem(model + d, halves) for d in range(1, halves)]

    def remote(source, target, send, receive, device):
        return pltpu.make_async_remote_copy(
            src_ref=source,
            dst_ref=target,
            send_sem=send,
            recv_sem=receive,
            device_id=device,
            device_id_type=pl.DeviceIdType.MESH,
        )

    barrier = pltpu.get_barrier_semaphore()
    targets = [{"seq": t} for t in others] + [{"mp": m} for m in models] + [twin, mate]
    for target in targets:
        pl.semaphore_signal(
            barrier, inc=1, device_id=target, device_id_type=pl.DeviceIdType.MESH
        )
    pl.semaphore_wait(barrier, len(targets))

    sends = []
    locals_ = []

    def go(copy):
        copy.start()
        sends.append(copy)

    for w in range(2):
        for d, t in enumerate(others):
            go(
                remote(
                    shards[w].at[part],
                    fulls[w].at[0, seq, part],
                    z_send.at[w, d],
                    z_recv.at[w, seq],
                    {"seq": t},
                )
            )
    for d, m in enumerate(models):
        go(remote(rows, all_rows.at[model], x_send.at[d], x_recv.at[model], {"mp": m}))
    for w in range(2):
        go(remote(shards[w], fulls[w].at[1, seq], o_send.at[w], o_recv.at[w], mate))
        copy = pltpu.make_async_copy(shards[w], fulls[w].at[0, seq], local_sem.at[w])
        copy.start()
        locals_.append(copy)
    copy = pltpu.make_async_copy(rows, all_rows.at[model], local_sem.at[2])
    copy.start()
    locals_.append(copy)

    for w in range(2):
        full = fulls[w]
        for d, t in enumerate(others):
            mine = full.at[0, t, part]
            remote(mine, mine, z_send.at[w, d], z_recv.at[w, t], {"seq": t}).wait_recv()
            go(remote(mine, mine, y_send.at[w, d], y_recv.at[w, t], twin))
            go(remote(mine, full.at[1, t, part], s_send.at[w, d, 0], s_recv.at[w, t, part], mate))
    for w in range(2):
        full = fulls[w]
        for d, t in enumerate(others):
            theirs = full.at[0, t, 1 - part]
            remote(theirs, theirs, y_send.at[w, d], y_recv.at[w, t], twin).wait_recv()
            go(
                remote(
                    theirs,
                    full.at[1, t, 1 - part],
                    s_send.at[w, d, 1],
                    s_recv.at[w, t, 1 - part],
                    mate,
                )
            )
    for w in range(2):
        full = fulls[w]
        own = full.at[1, seq]
        remote(own, own, o_send.at[w], o_recv.at[w], mate).wait_recv()
        for d, t in enumerate(others):
            for h in range(2):
                block = full.at[1, t, h]
                remote(block, block, s_send.at[w, d, h], s_recv.at[w, t, h], mate).wait_recv()
    for d, m in enumerate(models):
        block = all_rows.at[m]
        remote(block, block, x_send.at[d], x_recv.at[m], {"mp": m}).wait_recv()
    for copy in sends:
        copy.wait_send()
    for copy in locals_:
        copy.wait()


def gather_all(first, second, rows):
    peers, halves = (lax.axis_size("seq"), lax.axis_size("mp"))
    depth = first.shape[0] // 2
    shards = tuple(a.reshape(2, depth, -1) for a in (first, second))
    anywhere = pl.BlockSpec(memory_space=pl.ANY)
    dma = pltpu.SemaphoreType.DMA
    out = pl.pallas_call(
        partial(gather_kernel, peers, halves),
        out_shape=tuple(
            jax.ShapeDtypeStruct((2, peers) + a.shape, a.dtype) for a in shards
        )
        + (jax.ShapeDtypeStruct((halves,) + rows.shape, rows.dtype),),
        in_specs=[anywhere] * 3,
        out_specs=(anywhere,) * 3,
        scratch_shapes=[
            dma((3,)),
            dma((2, peers)),
            dma((2, peers)),
            dma((2, peers)),
            dma((2, peers)),
            dma((2, peers, 2)),
            dma((2, peers, 2)),
            dma((2,)),
            dma((2,)),
            dma((halves,)),
            dma((halves,)),
        ],
        compiler_params=pltpu.CompilerParams(collective_id=0, has_side_effects=True),
    )(*shards, rows)
    return (
        out[0].reshape(4 * peers * depth, -1),
        out[1].reshape(4 * peers * depth, -1),
        out[2],
    )


def exchange_kernel(peers, count, *refs):
    sources, targets = refs[:count], refs[count : 2 * count]
    local_sem, send_sem, recv_sem = refs[2 * count :]
    seq = lax.axis_index("seq")
    others = [lax.rem(seq + d, peers) for d in range(1, peers)]

    barrier = pltpu.get_barrier_semaphore()
    for t in others:
        pl.semaphore_signal(
            barrier, inc=1, device_id={"seq": t}, device_id_type=pl.DeviceIdType.MESH
        )
    pl.semaphore_wait(barrier, len(others))

    started = []
    for w in range(count):
        for d, t in enumerate(others):
            copy = pltpu.make_async_remote_copy(
                src_ref=sources[w].at[t],
                dst_ref=targets[w].at[seq],
                send_sem=send_sem.at[w, d],
                recv_sem=recv_sem.at[w, seq],
                device_id={"seq": t},
                device_id_type=pl.DeviceIdType.MESH,
            )
            copy.start()
            started.append(copy)
    own = [
        pltpu.make_async_copy(sources[w].at[seq], targets[w].at[seq], local_sem.at[w])
        for w in range(count)
    ]
    for copy in own:
        copy.start()
    for w in range(count):
        for d, t in enumerate(others):
            block = targets[w].at[t]
            pltpu.make_async_remote_copy(
                src_ref=block,
                dst_ref=block,
                send_sem=send_sem.at[w, d],
                recv_sem=recv_sem.at[w, t],
                device_id={"seq": t},
                device_id_type=pl.DeviceIdType.MESH,
            ).wait_recv()
    for copy in started:
        copy.wait_send()
    for copy in own:
        copy.wait()


def exchange(values):
    peers = lax.axis_size("seq")
    count = len(values)
    blocks = tuple(v.reshape(peers, v.shape[0] // peers, -1) for v in values)
    anywhere = pl.BlockSpec(memory_space=pl.ANY)
    dma = pltpu.SemaphoreType.DMA
    arrived = pl.pallas_call(
        partial(exchange_kernel, peers, count),
        out_shape=tuple(jax.ShapeDtypeStruct(v.shape, v.dtype) for v in blocks),
        in_specs=[anywhere] * count,
        out_specs=(anywhere,) * count,
        scratch_shapes=[dma((count,)), dma((count, peers)), dma((count, peers))],
        compiler_params=pltpu.CompilerParams(collective_id=1, has_side_effects=True),
    )(*blocks)
    return tuple(jnp.sum(v.astype(jnp.float32), axis=0) for v in arrived)


def core_sum(own, other):
    arrived = swap(other, "strand")
    return (own.astype(jnp.float32) + arrived.astype(jnp.float32)).astype(jnp.bfloat16)


def share_sum(own, other):
    return lax.psum_scatter(core_sum(own, other), "seq", scatter_dimension=0, tiled=True)


def on_device(
    hidden,
    breaks,
    cotangent,
    input_weight,
    gate_weight,
    key_weight,
    query_weight,
    step_weight,
    output_weight,
    step_bias,
    decay_log,
    skip_gain,
):
    strand = lax.axis_index("strand")
    backward = strand == 1
    seq_index = lax.axis_index("seq")
    length = hidden.shape[0]
    shard_rows = input_weight.shape[0]
    peers = lax.axis_size("seq")
    halves = lax.axis_size("mp")
    width = shard_rows * peers * 2
    half = shard_rows * peers
    part_width = hidden.shape[1]

    target = lax.broadcasted_iota(jnp.int32, (width, width), 1)
    source = lax.broadcasted_iota(jnp.int32, (width, width), 0)
    local = target % half
    side = jnp.where(target < half, strand, 1 - strand)
    feature = (local // shard_rows) * (2 * shard_rows) + side * shard_rows + local % shard_rows
    feature = jnp.where(backward, width - 1 - feature, feature)
    moves = (source == feature).astype(jnp.bfloat16)
    moves = lax.optimization_barrier(moves)

    key_width = key_weight.shape[1]
    inner_width = input_weight.shape[1]
    ahead = jnp.concatenate(
        (input_weight, gate_weight, key_weight, query_weight, step_weight), axis=1
    )
    ahead_full, out_full, everything = gather_all(
        ahead, output_weight, jnp.stack((hidden, cotangent))
    )

    def permuted(which):
        return sum(
            jnp.dot(
                everything[m, which],
                moves[m * part_width : (m + 1) * part_width],
                preferred_element_type=jnp.float32,
            )
            for m in range(halves)
        ).astype(jnp.bfloat16)

    inputs = permuted(0)
    grads_in = permuted(1)
    break_marks = lax.dynamic_slice_in_dim(breaks, seq_index * length, length).astype(jnp.float32)

    def project(start, size):
        return jnp.dot(
            inputs, ahead_full[:, start : start + size], preferred_element_type=jnp.float32
        )

    groups = key_width // STATE
    key_start = 2 * inner_width
    key_vals = project(key_start, key_width).astype(jnp.bfloat16).reshape(length, groups, STATE)
    query_vals = (
        project(key_start + key_width, key_width)
        .astype(jnp.bfloat16)
        .reshape(length, groups, STATE)
    )
    step_raw = project(key_start + 2 * key_width, step_weight.shape[1])
    inner_vals = project(0, inner_width).astype(jnp.bfloat16).reshape(length, -1, HEAD_DIM)
    gate_vals = project(inner_width, inner_width).astype(jnp.bfloat16).reshape(length, groups, -1)

    local_terms, local_pull = jax.vjp(
        partial(block_terms, backward, step_bias, decay_log, break_marks),
        inner_vals,
        key_vals,
        query_vals,
        step_raw,
    )
    total_log, total_state = local_terms[4:]
    head_shape = total_state.shape[:2]
    all_logs = lax.all_gather(total_log, "seq")
    order = earlier_than(peers, backward)
    chain = chain_weights(order, all_logs)
    here = lax.dynamic_index_in_dim(chain, seq_index, 0, keepdims=False)
    there = lax.dynamic_index_in_dim(chain, seq_index, 1, keepdims=False)

    def chained(value, weights):
        everything = lax.all_gather(value.astype(jnp.bfloat16), "seq")
        weights = weights.reshape((peers,) + head_shape)
        return sum(
            weights[k][..., None, None] * everything[k].astype(jnp.float32) for k in range(peers)
        )

    entering = chained(total_state, here)
    mixer_out, finish_pull = jax.vjp(
        partial(finish_terms, skip_gain), *local_terms[:4], query_vals, inner_vals, entering
    )
    gated, gate_pull = jax.vjp(gate_terms, mixer_out, gate_vals)
    gated_flat = gated.reshape(length, -1)

    gated_back = jnp.dot(grads_in, out_full, preferred_element_type=jnp.float32).astype(jnp.bfloat16).reshape(gated.shape)
    mixer_back, gate_back = gate_pull(gated_back)
    finish_back = finish_pull(mixer_back)
    carried_back = chained(finish_back[6], there)

    contract_rows = (((1,), (1,)), ((), ()))
    head_terms = tuple(
        lax.dot_general(
            gated_flat, part, contract_rows, preferred_element_type=jnp.float32
        ).astype(jnp.bfloat16)
        for part in (out_full[:half], out_full[half:])
    )
    head_terms = jnp.stack(
        [
            sum(
                lax.dot_general(
                    head_terms[s],
                    moves[m * part_width : (m + 1) * part_width, s * half : (s + 1) * half],
                    contract_rows,
                    preferred_element_type=jnp.float32,
                )
                for s in range(2)
            ).astype(jnp.bfloat16)
            for m in range(halves)
        ]
    )
    reduced = lax.psum_scatter(head_terms, "mp", scatter_dimension=0)
    combined = (
        reduced.astype(jnp.float32) + swap(reduced, "strand").astype(jnp.float32)
    ).astype(jnp.bfloat16)

    contract = (((0,), (0,)), ((), ()))

    def grad_pair(left, right):
        return tuple(
            lax.dot_general(part, right, contract, preferred_element_type=jnp.float32).astype(
                jnp.bfloat16
            )
            for part in (left[:, :half], left[:, half:])
        )

    grad_output = share_sum(*grad_pair(grads_in, gated_flat)).astype(jnp.float32)
    grad_gate = share_sum(*grad_pair(inputs, gate_back.reshape(length, -1))).astype(jnp.float32)

    log_back = jnp.sum(carried_back * entering, axis=(-2, -1)).reshape(
        total_log.shape
    ) * jnp.exp(total_log)
    local_back = local_pull((*finish_back[:4], log_back, carried_back))
    inner_back = (local_back[0] + finish_back[5]).reshape(length, -1)
    key_back = local_back[1].reshape(length, -1)
    query_back = (local_back[2] + finish_back[4]).reshape(length, -1)
    step_back = local_back[3]

    input_terms = grad_pair(inputs, inner_back)
    small_terms = tuple(
        jnp.concatenate(
            (
                lax.dot_general(
                    part, key_back, contract, preferred_element_type=jnp.float32
                ).astype(jnp.bfloat16),
                lax.dot_general(
                    part, query_back, contract, preferred_element_type=jnp.float32
                ).astype(jnp.bfloat16),
                lax.dot_general(
                    part.astype(jnp.float32), step_back, contract, precision=HIGHEST
                ).astype(jnp.bfloat16),
            ),
            axis=1,
        )
        for part in (inputs[:, :half], inputs[:, half:])
    )
    grad_input, small_share = exchange((core_sum(*input_terms), core_sum(*small_terms)))
    return (
        combined,
        grad_input,
        grad_gate,
        small_share[:, :key_width],
        small_share[:, key_width : 2 * key_width],
        small_share[:, 2 * key_width :],
        grad_output,
    )


def solution(mesh):
    in_specs = (
        P(("parts", "seq"), "mp"),
        P("parts"),
        P(("parts", "seq"), "mp"),
        P(("seq", "strand"), "mp"),
        P(("seq", "strand"), "mp"),
        P(("seq", "strand"), "mp"),
        P(("seq", "strand"), "mp"),
        P(("seq", "strand"), "mp"),
        P(("seq", "strand"), "mp"),
        P("mp"),
        P("mp"),
        P("mp"),
    )
    out_specs = (
        P(("parts", "seq"), "mp"),
        P(("parts", "seq", "strand"), "mp"),
        P(("parts", "seq", "strand"), "mp"),
        P(("parts", "seq", "strand"), "mp"),
        P(("parts", "seq", "strand"), "mp"),
        P(("parts", "seq", "strand"), "mp"),
        P(("parts", "seq", "strand"), "mp"),
    )
    return jax.shard_map(
        on_device, mesh=mesh, in_specs=in_specs, out_specs=out_specs, check_vma=False
    )
```

```python
from functools import partial

import jax
import jax.numpy as jnp
from jax import lax
from jax.experimental import pallas as pl
from jax.experimental.pallas import tpu as pltpu
from jax.sharding import PartitionSpec as P

HEAD_DIM = 64
STATE = 128
STRETCH = 256


KEEP_LOG = -0.35667494393873245
EPSILON = 1e-05
HIGHEST = lax.Precision.HIGHEST


def swap(value, axis):
    size = lax.axis_size(axis)
    return lax.ppermute(value, axis, [(i, size - 1 - i) for i in range(size)])


def earlier_than(count, backward):
    row = lax.broadcasted_iota(jnp.int32, (count, count), 0)
    column = lax.broadcasted_iota(jnp.int32, (count, count), 1)
    return jnp.where(backward, column > row, column < row)


def chain_weights(before, logs):
    steps = before.astype(jnp.float32)
    between = steps[:, None, :] * jnp.transpose(steps)[None, :, :]
    spans = jnp.sum(between[..., None] * logs[None, None], axis=2)
    return jnp.where(before[..., None], jnp.exp(spans), 0.0)


def block_terms(
    backward, step_bias, decay_log, break_marks, inner_vals, key_vals, query_vals, step_raw
):
    length = inner_vals.shape[0]
    blocks = length // STRETCH
    head_count = inner_vals.shape[1]
    groups = key_vals.shape[1]
    per_group = head_count // groups
    before = earlier_than(STRETCH, backward)
    row = lax.broadcasted_iota(jnp.int32, (STRETCH, STRETCH), 0)
    column = lax.broadcasted_iota(jnp.int32, (STRETCH, STRETCH), 1)
    causal = before | (row == column)
    step_size = jax.nn.softplus(step_raw + step_bias)
    log_rates = -jnp.exp(decay_log) * step_size + KEEP_LOG * break_marks[:, None]
    rate_rows = jnp.transpose(log_rates.reshape(blocks, STRETCH, head_count), (0, 2, 1))
    step_rows = jnp.transpose(step_size.reshape(blocks, STRETCH, head_count), (0, 2, 1))
    log_rows = jnp.einsum("chj,ij->chi", rate_rows, causal.astype(jnp.float32), precision=HIGHEST)
    ends = jnp.sum(rate_rows, axis=-1)
    end_rows = jnp.exp(ends[..., None] - log_rows) * step_rows
    log_decay = jnp.transpose(log_rows, (0, 2, 1))
    key_blocks = key_vals.reshape(blocks, STRETCH, groups, -1)
    query_blocks = query_vals.reshape(blocks, STRETCH, groups, -1)
    inner_blocks = inner_vals.reshape(blocks, STRETCH, groups, per_group, -1)
    scores = jnp.einsum(
        "cqgn,ckgn->cgqk", query_blocks, key_blocks, preferred_element_type=jnp.float32
    )
    decay_rows = log_rows.reshape(blocks, groups, per_group, STRETCH)
    step_heads = step_rows.reshape(blocks, groups, per_group, STRETCH)
    spread = decay_rows[..., :, None] - decay_rows[..., None, :]
    within = jnp.where(causal, jnp.exp(jnp.where(causal, spread, 0.0)), 0.0)
    mixing = (scores[:, :, None] * within * step_heads[..., None, :]).astype(jnp.bfloat16)
    local_out = jnp.einsum(
        "cghqk,ckghp->cqghp", mixing, inner_blocks, preferred_element_type=jnp.float32
    )
    to_end = jnp.transpose(end_rows, (0, 2, 1)).reshape(blocks, STRETCH, groups, per_group)
    weighted = (inner_blocks * to_end[..., None]).astype(jnp.bfloat16)
    block_states = jnp.einsum(
        "cqghp,cqgn->cghpn", weighted, key_blocks, preferred_element_type=jnp.float32
    )
    order = earlier_than(blocks, backward)
    head_shape = (groups, per_group)
    weights = chain_weights(order, ends).reshape((blocks, blocks) + head_shape)
    prior_state = jnp.stack(
        [
            sum(
                weights[c, k][..., None, None] * block_states[k] for k in range(blocks) if k != c
            )
            if blocks > 1
            else jnp.zeros_like(block_states[0])
            for c in range(blocks)
        ]
    )
    order_f = order.astype(jnp.float32)
    prior_logs = jnp.sum(order_f[:, :, None] * ends[None], axis=1)
    later_logs = jnp.sum(jnp.transpose(order_f)[:, :, None] * ends[None], axis=1)
    prior_decay = jnp.exp(prior_logs).reshape((blocks,) + head_shape)
    later_decay = jnp.exp(later_logs).reshape((blocks,) + head_shape)
    total_state = sum(later_decay[c][..., None, None] * block_states[c] for c in range(blocks))
    total_log = jnp.sum(ends, axis=0)
    return (local_out, prior_state, prior_decay, log_decay, total_log, total_state)


def finish_terms(
    skip_gain,
    local_out,
    prior_state,
    prior_decay,
    log_decay,
    query_vals,
    inner_vals,
    entering,
):
    blocks = log_decay.shape[0]
    groups = query_vals.shape[1]
    per_group = inner_vals.shape[1] // groups
    states = prior_state + prior_decay[..., None, None] * entering
    query_full = query_vals.reshape(blocks, STRETCH, groups, -1).astype(jnp.float32)
    carried = jnp.einsum("cqgn,cghpn->cqghp", query_full, states, precision=HIGHEST)
    growth = jnp.exp(log_decay).reshape(blocks, STRETCH, groups, per_group)
    inner_full = inner_vals.reshape(blocks, STRETCH, groups, per_group, -1).astype(jnp.float32)
    mixer_out = (
        local_out
        + growth[..., None] * carried
        + skip_gain.reshape(groups, per_group)[:, :, None] * inner_full
    )
    return mixer_out.reshape(blocks * STRETCH, groups, -1)


def gate_terms(mixer_out, gate_vals):
    product = mixer_out * jax.nn.silu(gate_vals.astype(jnp.float32))
    scaled = product * lax.rsqrt(jnp.mean(product * product, axis=-1, keepdims=True) + EPSILON)
    return scaled.astype(jnp.bfloat16)


def gather_kernel(peers, halves, *refs):
    shards, rows, fulls, all_rows = refs[:2], refs[2], refs[3:5], refs[5]
    local_sem, z_send, z_recv, y_send, y_recv, s_send, s_recv, o_send, o_recv, x_send, x_recv = refs[6:]
    part = lax.axis_index("parts")
    seq = lax.axis_index("seq")
    strand = lax.axis_index("strand")
    model = lax.axis_index("mp")
    twin = {"parts": 1 - part}
    mate = {"strand": 1 - strand}
    others = [lax.rem(seq + d, peers) for d in range(1, peers)]
    models = [lax.rem(model + d, halves) for d in range(1, halves)]

    def remote(source, target, send, receive, device):
        return pltpu.make_async_remote_copy(
            src_ref=source,
            dst_ref=target,
            send_sem=send,
            recv_sem=receive,
            device_id=device,
            device_id_type=pl.DeviceIdType.MESH,
        )

    barrier = pltpu.get_barrier_semaphore()
    targets = [{"seq": t} for t in others] + [{"mp": m} for m in models] + [twin, mate]
    for target in targets:
        pl.semaphore_signal(
            barrier, inc=1, device_id=target, device_id_type=pl.DeviceIdType.MESH
        )
    pl.semaphore_wait(barrier, len(targets))

    sends = []
    locals_ = []

    def go(copy):
        copy.start()
        sends.append(copy)

    for w in range(2):
        for d, t in enumerate(others):
            go(
                remote(
                    shards[w].at[part],
                    fulls[w].at[0, seq, part],
                    z_send.at[w, d],
                    z_recv.at[w, seq],
                    {"seq": t},
                )
            )
    for d, m in enumerate(models):
        go(remote(rows, all_rows.at[model], x_send.at[d], x_recv.at[model], {"mp": m}))
    for w in range(2):
        go(remote(shards[w], fulls[w].at[1, seq], o_send.at[w], o_recv.at[w], mate))
        copy = pltpu.make_async_copy(shards[w], fulls[w].at[0, seq], local_sem.at[w])
        copy.start()
        locals_.append(copy)
    copy = pltpu.make_async_copy(rows, all_rows.at[model], local_sem.at[2])
    copy.start()
    locals_.append(copy)

    for w in range(2):
        full = fulls[w]
        for d, t in enumerate(others):
            mine = full.at[0, t, part]
            remote(mine, mine, z_send.at[w, d], z_recv.at[w, t], {"seq": t}).wait_recv()
            go(remote(mine, mine, y_send.at[w, d], y_recv.at[w, t], twin))
            go(remote(mine, full.at[1, t, part], s_send.at[w, d, 0], s_recv.at[w, t, part], mate))
    for w in range(2):
        full = fulls[w]
        for d, t in enumerate(others):
            theirs = full.at[0, t, 1 - part]
            remote(theirs, theirs, y_send.at[w, d], y_recv.at[w, t], twin).wait_recv()
            go(
                remote(
                    theirs,
                    full.at[1, t, 1 - part],
                    s_send.at[w, d, 1],
                    s_recv.at[w, t, 1 - part],
                    mate,
                )
            )
    for w in range(2):
        full = fulls[w]
        own = full.at[1, seq]
        remote(own, own, o_send.at[w], o_recv.at[w], mate).wait_recv()
        for d, t in enumerate(others):
            for h in range(2):
                block = full.at[1, t, h]
                remote(block, block, s_send.at[w, d, h], s_recv.at[w, t, h], mate).wait_recv()
    for d, m in enumerate(models):
        block = all_rows.at[m]
        remote(block, block, x_send.at[d], x_recv.at[m], {"mp": m}).wait_recv()
    for copy in sends:
        copy.wait_send()
    for copy in locals_:
        copy.wait()


def gather_all(first, second, rows):
    peers, halves = (lax.axis_size("seq"), lax.axis_size("mp"))
    depth = first.shape[0] // 2
    shards = tuple(a.reshape(2, depth, -1) for a in (first, second))
    anywhere = pl.BlockSpec(memory_space=pl.ANY)
    dma = pltpu.SemaphoreType.DMA
    out = pl.pallas_call(
        partial(gather_kernel, peers, halves),
        out_shape=tuple(
            jax.ShapeDtypeStruct((2, peers) + a.shape, a.dtype) for a in shards
        )
        + (jax.ShapeDtypeStruct((halves,) + rows.shape, rows.dtype),),
        in_specs=[anywhere] * 3,
        out_specs=(anywhere,) * 3,
        scratch_shapes=[
            dma((3,)),
            dma((2, peers)),
            dma((2, peers)),
            dma((2, peers)),
            dma((2, peers)),
            dma((2, peers, 2)),
            dma((2, peers, 2)),
            dma((2,)),
            dma((2,)),
            dma((halves,)),
            dma((halves,)),
        ],
        compiler_params=pltpu.CompilerParams(collective_id=0, has_side_effects=True),
    )(*shards, rows)
    return (
        out[0].reshape(4 * peers * depth, -1),
        out[1].reshape(4 * peers * depth, -1),
        out[2],
    )


def exchange_kernel(peers, count, *refs):
    sources, targets = refs[:count], refs[count : 2 * count]
    local_sem, send_sem, recv_sem = refs[2 * count :]
    seq = lax.axis_index("seq")
    others = [lax.rem(seq + d, peers) for d in range(1, peers)]

    barrier = pltpu.get_barrier_semaphore()
    for t in others:
        pl.semaphore_signal(
            barrier, inc=1, device_id={"seq": t}, device_id_type=pl.DeviceIdType.MESH
        )
    pl.semaphore_wait(barrier, len(others))

    started = []
    for w in range(count):
        for d, t in enumerate(others):
            copy = pltpu.make_async_remote_copy(
                src_ref=sources[w].at[t],
                dst_ref=targets[w].at[seq],
                send_sem=send_sem.at[w, d],
                recv_sem=recv_sem.at[w, seq],
                device_id={"seq": t},
                device_id_type=pl.DeviceIdType.MESH,
            )
            copy.start()
            started.append(copy)
    own = [
        pltpu.make_async_copy(sources[w].at[seq], targets[w].at[seq], local_sem.at[w])
        for w in range(count)
    ]
    for copy in own:
        copy.start()
    for w in range(count):
        for d, t in enumerate(others):
            block = targets[w].at[t]
            pltpu.make_async_remote_copy(
                src_ref=block,
                dst_ref=block,
                send_sem=send_sem.at[w, d],
                recv_sem=recv_sem.at[w, t],
                device_id={"seq": t},
                device_id_type=pl.DeviceIdType.MESH,
            ).wait_recv()
    for copy in started:
        copy.wait_send()
    for copy in own:
        copy.wait()


def exchange(values):
    peers = lax.axis_size("seq")
    count = len(values)
    blocks = tuple(v.reshape(peers, v.shape[0] // peers, -1) for v in values)
    anywhere = pl.BlockSpec(memory_space=pl.ANY)
    dma = pltpu.SemaphoreType.DMA
    arrived = pl.pallas_call(
        partial(exchange_kernel, peers, count),
        out_shape=tuple(jax.ShapeDtypeStruct(v.shape, v.dtype) for v in blocks),
        in_specs=[anywhere] * count,
        out_specs=(anywhere,) * count,
        scratch_shapes=[dma((count,)), dma((count, peers)), dma((count, peers))],
        compiler_params=pltpu.CompilerParams(collective_id=1, has_side_effects=True),
    )(*blocks)
    return tuple(jnp.sum(v.astype(jnp.float32), axis=0) for v in arrived)


def core_sum(own, other):
    arrived = swap(other, "strand")
    return (own.astype(jnp.float32) + arrived.astype(jnp.float32)).astype(jnp.bfloat16)


def share_sum(own, other):
    return lax.psum_scatter(core_sum(own, other), "seq", scatter_dimension=0, tiled=True)


def on_device(
    hidden,
    breaks,
    cotangent,
    input_weight,
    gate_weight,
    key_weight,
    query_weight,
    step_weight,
    output_weight,
    step_bias,
    decay_log,
    skip_gain,
):
    strand = lax.axis_index("strand")
    backward = strand == 1
    seq_index = lax.axis_index("seq")
    length = hidden.shape[0]
    shard_rows = input_weight.shape[0]
    peers = lax.axis_size("seq")
    halves = lax.axis_size("mp")
    width = shard_rows * peers * 2
    half = shard_rows * peers
    part_width = hidden.shape[1]

    target = lax.broadcasted_iota(jnp.int32, (width, width), 1)
    source = lax.broadcasted_iota(jnp.int32, (width, width), 0)
    local = target % half
    side = jnp.where(target < half, strand, 1 - strand)
    feature = (local // shard_rows) * (2 * shard_rows) + side * shard_rows + local % shard_rows
    feature = jnp.where(backward, width - 1 - feature, feature)
    moves = (source == feature).astype(jnp.bfloat16)
    moves = lax.optimization_barrier(moves)

    key_width = key_weight.shape[1]
    inner_width = input_weight.shape[1]
    ahead = jnp.concatenate(
        (input_weight, gate_weight, key_weight, query_weight, step_weight), axis=1
    )
    ahead_full, out_full, everything = gather_all(
        ahead, output_weight, jnp.stack((hidden, cotangent))
    )

    def permuted(which):
        return sum(
            jnp.dot(
                everything[m, which],
                moves[m * part_width : (m + 1) * part_width],
                preferred_element_type=jnp.float32,
            )
            for m in range(halves)
        ).astype(jnp.bfloat16)

    inputs = permuted(0)
    grads_in = permuted(1)
    break_marks = lax.dynamic_slice_in_dim(breaks, seq_index * length, length).astype(jnp.float32)

    def project(start, size):
        return jnp.dot(
            inputs, ahead_full[:, start : start + size], preferred_element_type=jnp.float32
        )

    groups = key_width // STATE
    key_start = 2 * inner_width
    key_vals = project(key_start, key_width).astype(jnp.bfloat16).reshape(length, groups, STATE)
    query_vals = (
        project(key_start + key_width, key_width)
        .astype(jnp.bfloat16)
        .reshape(length, groups, STATE)
    )
    step_raw = project(key_start + 2 * key_width, step_weight.shape[1])
    inner_vals = project(0, inner_width).astype(jnp.bfloat16).reshape(length, -1, HEAD_DIM)
    gate_vals = project(inner_width, inner_width).astype(jnp.bfloat16).reshape(length, groups, -1)

    local_terms, local_pull = jax.vjp(
        partial(block_terms, backward, step_bias, decay_log, break_marks),
        inner_vals,
        key_vals,
        query_vals,
        step_raw,
    )
    total_log, total_state = local_terms[4:]
    head_shape = total_state.shape[:2]
    heads = total_log.shape[0]
    log_pieces = []
    rest = total_log
    for _ in range(3):
        piece = lax.reduce_precision(rest, 8, 7)
        log_pieces.append(piece)
        rest = rest - piece
    log_rows = jnp.pad(jnp.stack(log_pieces), ((0, 13), (0, STATE - heads)))
    sent = jnp.concatenate(
        (total_state.reshape(-1, STATE).astype(jnp.bfloat16), log_rows.astype(jnp.bfloat16))
    )
    arrived = lax.all_gather(sent, "seq")
    state_rows = heads * HEAD_DIM
    all_logs = jnp.sum(arrived[:, state_rows : state_rows + 3, :heads].astype(jnp.float32), axis=1)
    order = earlier_than(peers, backward)
    chain = chain_weights(order, all_logs)
    here = lax.dynamic_index_in_dim(chain, seq_index, 0, keepdims=False)
    there = lax.dynamic_index_in_dim(chain, seq_index, 1, keepdims=False)

    def chained(everything, weights):
        weights = weights.reshape((peers,) + head_shape)
        return sum(
            weights[k][..., None, None]
            * everything[k].reshape(total_state.shape).astype(jnp.float32)
            for k in range(peers)
        )

    entering = chained(arrived[:, :state_rows], here)
    mixer_out, finish_pull = jax.vjp(
        partial(finish_terms, skip_gain), *local_terms[:4], query_vals, inner_vals, entering
    )
    gated, gate_pull = jax.vjp(gate_terms, mixer_out, gate_vals)
    gated_flat = gated.reshape(length, -1)

    gated_back = jnp.dot(grads_in, out_full, preferred_element_type=jnp.float32).astype(jnp.bfloat16).reshape(gated.shape)
    mixer_back, gate_back = gate_pull(gated_back)
    finish_back = finish_pull(mixer_back)
    carried_back = chained(lax.all_gather(finish_back[6].astype(jnp.bfloat16), "seq"), there)

    contract_rows = (((1,), (1,)), ((), ()))
    head_terms = tuple(
        lax.dot_general(
            gated_flat, part, contract_rows, preferred_element_type=jnp.float32
        ).astype(jnp.bfloat16)
        for part in (out_full[:half], out_full[half:])
    )
    head_terms = jnp.stack(
        [
            sum(
                lax.dot_general(
                    head_terms[s],
                    moves[m * part_width : (m + 1) * part_width, s * half : (s + 1) * half],
                    contract_rows,
                    preferred_element_type=jnp.float32,
                )
                for s in range(2)
            ).astype(jnp.bfloat16)
            for m in range(halves)
        ]
    )
    reduced = lax.psum_scatter(head_terms, "mp", scatter_dimension=0)
    combined = (
        reduced.astype(jnp.float32) + swap(reduced, "strand").astype(jnp.float32)
    ).astype(jnp.bfloat16)

    contract = (((0,), (0,)), ((), ()))

    def grad_pair(left, right):
        return tuple(
            lax.dot_general(part, right, contract, preferred_element_type=jnp.float32).astype(
                jnp.bfloat16
            )
            for part in (left[:, :half], left[:, half:])
        )

    grad_output = share_sum(*grad_pair(grads_in, gated_flat)).astype(jnp.float32)
    grad_gate = share_sum(*grad_pair(inputs, gate_back.reshape(length, -1))).astype(jnp.float32)

    log_back = jnp.sum(carried_back * entering, axis=(-2, -1)).reshape(
        total_log.shape
    ) * jnp.exp(total_log)
    local_back = local_pull((*finish_back[:4], log_back, carried_back))
    inner_back = (local_back[0] + finish_back[5]).reshape(length, -1)
    key_back = local_back[1].reshape(length, -1)
    query_back = (local_back[2] + finish_back[4]).reshape(length, -1)
    step_back = local_back[3]

    input_terms = grad_pair(inputs, inner_back)
    small_terms = tuple(
        jnp.concatenate(
            (
                lax.dot_general(
                    part, key_back, contract, preferred_element_type=jnp.float32
                ).astype(jnp.bfloat16),
                lax.dot_general(
                    part, query_back, contract, preferred_element_type=jnp.float32
                ).astype(jnp.bfloat16),
                lax.dot_general(
                    part.astype(jnp.float32), step_back, contract, precision=HIGHEST
                ).astype(jnp.bfloat16),
            ),
            axis=1,
        )
        for part in (inputs[:, :half], inputs[:, half:])
    )
    grad_input, small_share = exchange((core_sum(*input_terms), core_sum(*small_terms)))
    return (
        combined,
        grad_input,
        grad_gate,
        small_share[:, :key_width],
        small_share[:, key_width : 2 * key_width],
        small_share[:, 2 * key_width :],
        grad_output,
    )


def solution(mesh):
    in_specs = (
        P(("parts", "seq"), "mp"),
        P("parts"),
        P(("parts", "seq"), "mp"),
        P(("seq", "strand"), "mp"),
        P(("seq", "strand"), "mp"),
        P(("seq", "strand"), "mp"),
        P(("seq", "strand"), "mp"),
        P(("seq", "strand"), "mp"),
        P(("seq", "strand"), "mp"),
        P("mp"),
        P("mp"),
        P("mp"),
    )
    out_specs = (
        P(("parts", "seq"), "mp"),
        P(("parts", "seq", "strand"), "mp"),
        P(("parts", "seq", "strand"), "mp"),
        P(("parts", "seq", "strand"), "mp"),
        P(("parts", "seq", "strand"), "mp"),
        P(("parts", "seq", "strand"), "mp"),
        P(("parts", "seq", "strand"), "mp"),
    )
    return jax.shard_map(
        on_device, mesh=mesh, in_specs=in_specs, out_specs=out_specs, check_vma=False
    )
```
